32 devices in a mesh: space: 8 (over z, y), species: 4 (over x, core).
Axes of the slice: x: 2, y: 2, z: 4, core: 2. Of those that a mesh axis runs over, the one named last changes fastest.
Arguments:
- effects: float32 [48, 256, 2048], P('space', None, 'species'), may hold values from -1.2 to 1.2
- kappa_sq: float32 [48, 256], P('space'), may hold values from 0.1 to 2
- growth: float32 [48, 256, 128], P('space'), may hold values from -6 to 6
- tree_species: int32 [48, 256, 128], P('space'), may hold values from 0 to 2047
- tree_counts: int32 [48, 256], P('space'), may hold values from 1 to 128, as said below
- noise_precision: float32 [2048], P('species'), may hold values from 0.5 to 4
- species_precision: bfloat16 [2048, 2048], P(None, 'species'), as said below
Outputs:
- grad_effects: float32 [48, 256, 2048], P('space', None, 'species')
- gram: float32 [2048, 2048], P('space', 'species')
The draws below stay inside these ranges and needn't reach their ends.
Inputs may be any that keep to these rules, and one draw needn't show every extreme that they name: `tree_counts`: some plot has 128 live trees. species_precision is symmetric.
All inputs are finite; a program needn't handle non-finite values.
Results may differ from the reference program's by a relative error of at most 0.0029.
Values may be sent and summed in bfloat16 or wider, within the bound.
No kernel may reach another device: no remote copies, remote signals or barrier semaphores. Data moves between devices by JAX's collectives and lax.ppermute only.
A program may use at most 128 MiB of HBM per device.

```python
import math
import jax
import jax.numpy as jnp
import numpy as np
from jax import lax

S = 2048
GC = 256
TREES = 128
GRID_R = 48
NPLOTS = 12288


def draw_tree_counts(key, part):
    drawn_counts = jax.random.randint(key, (GRID_R, GC), 1, TREES + 1)
    flat_index = lax.broadcasted_iota(jnp.int32, (GRID_R, GC), 0) * GC + lax.broadcasted_iota(jnp.int32, (GRID_R, GC), 1)
    return jnp.where(flat_index % 64 == 0, TREES, drawn_counts).astype(jnp.int32)


def draw_species_precision(key, part):
    first_key, second_key = jax.random.split(jax.random.fold_in(key, 7))
    base_draw = jax.random.normal(first_key, (S, S), jnp.float32)
    diagonal_draw = jax.random.uniform(second_key, (S,), jnp.float32, 1.0, 2.0)
    identity = (lax.broadcasted_iota(jnp.int32, (S, S), 0) == lax.broadcasted_iota(jnp.int32, (S, S), 1)).astype(jnp.float32)
    off_part = (base_draw + base_draw.T) * (0.25 / math.sqrt(S))
    result_matrix = off_part * (1.0 - identity) + identity * diagonal_draw[:, None]
    return result_matrix.astype(jnp.bfloat16)


def set_ends(drawn, stream_key, smallest, largest):
    longest = drawn.shape.index(max(drawn.shape))
    spots = []
    for shift in (0, 1):
        where = [jax.random.randint(jax.random.fold_in(stream_key, axis), (), 0, length) for axis, length in enumerate(drawn.shape)]
        where[longest] = (where[longest] + shift) % drawn.shape[longest]
        spots.append(tuple(where))
    return drawn.at[spots[0]].set(smallest).at[spots[1]].set(largest)


def block_levels(stream_key, shape, shards, smallest, high):
    def one(axis_at, blocks):
        draws = jax.random.uniform(jax.random.fold_in(jax.random.fold_in(stream_key, 6), axis_at), (blocks,), jnp.float32, smallest / len(shards), high / len(shards))
        return jnp.repeat(jnp.exp(draws), shape[axis_at] // blocks).reshape((-1,) + (1,) * (len(shape) - axis_at - 1))

    level = one(*shards[0])
    for cut in shards[1:]:
        level = level * one(*cut)
    return level


def rank_bounds(number_of, slope):
    loads = [(1 << 20) // math.isqrt(grade ** slope) + 1 for grade in range(1, number_of + 1)]
    width = 1 + sum(loads) // (1 << 30)
    return np.cumsum(np.array([max(1, weight // width) for weight in loads]))


def skewed_ids(rng, shape, number_of, slope):
    table = rank_bounds(number_of, slope)
    ticket = jax.random.randint(jax.random.fold_in(rng, 1), shape, 0, int(table[number_of - 1]))
    standing = jnp.searchsorted(jnp.asarray(table, jnp.int32), ticket, side="right")
    return jax.random.permutation(jax.random.fold_in(rng, 2), number_of)[standing].astype(jnp.int32)


def centred(own_key, extent, deviation, most, cuts=(), kind=jnp.bfloat16):
    array = deviation * jax.random.normal(own_key, extent, jnp.float32)
    if cuts:
        array = array * block_levels(own_key, extent, cuts, -0.22, 0.18)
    return jnp.clip(array, -most, most).astype(kind)


def setup_inputs(seed: int = 0) -> dict:
    key_of = jax.random.split(jax.random.key(seed), 8)
    effects = centred(key_of[0], (GRID_R, GC, S), 0.2, 1.2, ((0, 8), (2, 4)), jnp.float32)
    kappa_sq = jnp.clip(jnp.exp(math.log(2.0) - 2.9957323 * jax.random.uniform(key_of[1], (GRID_R, GC), jnp.float32) ** block_levels(key_of[1], (GRID_R, GC), ((0, 8),), -0.2, 0.2)), 0.1, 2.0)
    growth = centred(key_of[2], (GRID_R, GC, TREES), 1.0, 6.0, ((0, 8),), jnp.float32)
    tree_species = set_ends(skewed_ids(key_of[3], (GRID_R, GC, TREES), S, 2), jax.random.fold_in(key_of[3], 3), 0, S - 1).astype(jnp.int32)
    tree_counts = draw_tree_counts(jax.random.fold_in(key_of[7], 71), 0)
    noise_precision = jnp.clip(jnp.exp(math.log(4.0) - 2.0794415 * jax.random.uniform(key_of[5], (S,), jnp.float32) ** block_levels(key_of[5], (S,), ((0, 4),), -0.2, 0.2)), 0.5, 4.0)
    species_precision = draw_species_precision(jax.random.fold_in(key_of[7], 71), 0)
    return dict(effects=effects, kappa_sq=kappa_sq, growth=growth, tree_species=tree_species, tree_counts=tree_counts, noise_precision=noise_precision, species_precision=species_precision)


def apply_k(field_in, kappa_grid):
    padded = jnp.pad(field_in, ((1, 1), (1, 1), (0, 0)))
    beside = padded[2:, 1:-1] + padded[:-2, 1:-1] + padded[1:-1, 2:] + padded[1:-1, :-2]
    return (kappa_grid[..., None] + 4.0) * field_in - beside


def reference(effects, kappa_sq, growth, tree_species, tree_counts, noise_precision, species_precision):
    spatial = apply_k(apply_k(effects, kappa_sq), kappa_sq)
    spatial_low = spatial.astype(jnp.bfloat16).astype(jnp.float32).reshape(NPLOTS, S)
    effects_low = effects.astype(jnp.bfloat16).astype(jnp.float32).reshape(NPLOTS, S)
    precision_wide = species_precision.astype(jnp.float32)
    prior_term = jnp.dot(spatial_low, precision_wide, precision=lax.Precision.HIGHEST)
    growth_low = growth.astype(jnp.bfloat16).astype(jnp.float32)
    live_tree = lax.broadcasted_iota(jnp.int32, (GRID_R, GC, TREES), 2) < tree_counts[..., None]
    plot_index = lax.broadcasted_iota(jnp.int32, (NPLOTS, TREES), 0)
    species_flat = tree_species.reshape(NPLOTS, TREES)
    live_flat = live_tree.reshape(NPLOTS, TREES)
    growth_sum = jnp.zeros((NPLOTS, S), jnp.float32).at[plot_index, species_flat].add(jnp.where(live_flat, growth_low.reshape(NPLOTS, TREES), jnp.float32(0.0)))
    tally = jnp.zeros((NPLOTS, S), jnp.float32).at[plot_index, species_flat].add(jnp.where(live_flat, jnp.float32(1.0), jnp.float32(0.0)))
    grad_flat = noise_precision[None, :] * (growth_sum - tally * effects.reshape(NPLOTS, S)) - prior_term
    gram = jnp.dot(effects_low.T, spatial_low, precision=lax.Precision.HIGHEST) * (-0.5 / NPLOTS)
    return grad_flat.reshape(GRID_R, GC, S), gram
```

```python
import functools

import jax
import jax.numpy as jnp
from jax import lax
from jax.experimental import pallas as pl
from jax.experimental.pallas import tpu as pltpu
from jax.sharding import PartitionSpec as P


LANES = 128


def xor_swap(value, axis, mask):
    count = lax.axis_size(axis)
    return lax.ppermute(value, axis, [(i, i ^ mask) for i in range(count)])


def tree_kernel(groups, first_ref, effects_ref, growth_ref, species_ref, counts_ref, noise_ref, *rest):
    out_ref = rest[-1]
    rows, slots = growth_ref.shape
    bits = LANES.bit_length() - 1
    codes = groups * 8
    low_iota = lax.broadcasted_iota(jnp.int32, (LANES, slots), 0).astype(jnp.bfloat16)
    code_iota = lax.broadcasted_iota(jnp.int32, (codes, slots), 0).astype(jnp.bfloat16)
    slot_iota = lax.broadcasted_iota(jnp.int32, (8, slots), 1)
    row_iota = lax.broadcasted_iota(jnp.int32, (8, slots), 0)
    one, zero = jnp.bfloat16(1.0), jnp.bfloat16(0.0)
    first_column = first_ref[0]

    def step(index, carry):
        at = pl.ds(pl.multiple_of(index * 8, 8), 8)
        local = species_ref[at, :] - first_column
        group = local >> bits
        valid = (slot_iota < counts_ref[at, :]) & (group >= 0) & (group < groups)
        code = jnp.where(valid, group * 8 + row_iota, -1).astype(jnp.float32)
        low = (local & (LANES - 1)).astype(jnp.float32)
        value = growth_ref[at, :].astype(jnp.bfloat16).astype(jnp.float32)
        lefts, rights = [], []
        for plot in range(8):
            low_row = jnp.broadcast_to(low[plot : plot + 1], (LANES, slots)).astype(jnp.bfloat16)
            code_row = jnp.broadcast_to(code[plot : plot + 1], (codes, slots)).astype(jnp.bfloat16)
            value_row = jnp.broadcast_to(value[plot : plot + 1], (codes, slots)).astype(jnp.bfloat16)
            match = code_row == code_iota
            rights.append(jnp.where(low_row == low_iota, one, zero))
            lefts.append(
                jnp.concatenate([jnp.where(match, value_row, zero), jnp.where(match, one, zero)], axis=0)
            )
        sums = lax.dot_general(
            jnp.concatenate(lefts, axis=1),
            jnp.concatenate(rights, axis=1),
            (((1,), (1,)), ((), ())),
            preferred_element_type=jnp.float32,
        )
        for group_at in range(groups):
            cols = pl.ds(group_at * LANES, LANES)
            growth_sum = sums[group_at * 8 : group_at * 8 + 8]
            tally = sums[codes + group_at * 8 : codes + group_at * 8 + 8]
            out_ref[at, cols] = noise_ref[:, cols] * (growth_sum - tally * effects_ref[at, cols])
        return carry

    lax.fori_loop(0, rows // 8, step, 0, unroll=16)


def tree_term(effects, growth, species, counts, noise, first_column, start, length, before):
    plots, columns = effects.shape
    slots = growth.shape[1]
    block = 128
    first = start // block
    row = lambda width: pl.BlockSpec((block, width), lambda i: (first + i, 0))
    held = [] if before is None else [before]
    return pl.pallas_call(
        functools.partial(tree_kernel, columns // LANES),
        grid=(length // block,),
        in_specs=[
            pl.BlockSpec(memory_space=pltpu.SMEM),
            row(columns),
            row(slots),
            row(slots),
            row(1),
            pl.BlockSpec((1, columns), lambda i: (0, 0)),
        ]
        + [pl.BlockSpec(memory_space=pl.ANY)] * len(held),
        out_specs=row(columns),
        out_shape=jax.ShapeDtypeStruct((plots, columns), jnp.float32),
        input_output_aliases={6: 0} if held else {},
        cost_estimate=pl.CostEstimate(
            flops=2 * length * slots * 64 * 128, bytes_accessed=8 * length * (slots + columns), transcendentals=0
        ),
        name="tree_term",
    )(first_column.reshape(1), effects, growth, species, counts.reshape(plots, 1), noise.reshape(1, columns), *held)


def k_row(above, centre, below, kappa):
    at = lax.broadcasted_iota(jnp.int32, centre.shape, 0)
    last = centre.shape[0] - 1
    left = jnp.where(at == 0, 0.0, pltpu.roll(centre, 1, axis=0))
    right = jnp.where(at == last, 0.0, pltpu.roll(centre, last, axis=0))
    return (kappa + 4.0) * centre - (below + above + right + left)


def mid_kernel(rows, with_wide, *refs):
    if with_wide:
        x_ref, kappa_ref, low_ref, wide_ref = refs
        get = lambda r: x_ref[r]
    else:
        x_ref, top_ref, bottom_ref, kappa_ref, low_ref = refs
        get = lambda r: top_ref[0] if r == 0 else bottom_ref[0] if r == rows - 1 else x_ref[r - 1]
    for r in range(1, rows - 1):
        value = k_row(get(r - 1), get(r), get(r + 1), kappa_ref[r])
        low_ref[r - 1] = value.astype(low_ref.dtype)
        if with_wide:
            wide_ref[r - 1] = value


def edge_kernel(with_wide, above_ref, first_ref, second_ref, before_ref, last_ref, below_ref, kappa_ref, *outs):
    rows = kappa_ref.shape[0]
    top = k_row(above_ref[0], first_ref[0], second_ref[0], kappa_ref[0])
    bottom = k_row(before_ref[0], last_ref[0], below_ref[0], kappa_ref[rows - 1])
    for at, value in enumerate((top, bottom)):
        outs[0][at] = value.astype(outs[0].dtype)
        if with_wide:
            outs[1 + at][0] = value


def rows_spec(count, cols, first=0):
    return pl.BlockSpec((count, cols, LANES), lambda j: (first // count, 0, j))


def stencil_mid(x, edges, kappa, with_wide):
    rows, cols = kappa.shape[:2]
    columns = x.shape[2]
    shape = (rows - 2, cols, columns)
    outs = [jax.ShapeDtypeStruct(shape, jnp.bfloat16)]
    if with_wide:
        outs.append(jax.ShapeDtypeStruct(shape, jnp.float32))
    arrays = [x, *edges]
    return pl.pallas_call(
        functools.partial(mid_kernel, rows, with_wide),
        grid=(columns // LANES,),
        in_specs=[rows_spec(a.shape[0], cols) for a in arrays] + [pl.BlockSpec((rows, cols, 1), lambda j: (0, 0, 0))],
        out_specs=[rows_spec(rows - 2, cols) for _ in outs],
        out_shape=outs,
        cost_estimate=pl.CostEstimate(flops=8 * x.size, bytes_accessed=10 * x.size, transcendentals=0),
        name="stencil_mid",
    )(*arrays, kappa)


def stencil_edge(above, first, second, before, last, below, kappa, with_wide):
    rows, cols = kappa.shape[:2]
    columns = above.shape[2]
    outs = [jax.ShapeDtypeStruct((2, cols, columns), jnp.bfloat16)]
    if with_wide:
        outs += [jax.ShapeDtypeStruct((1, cols, columns), jnp.float32)] * 2
    picks = [(above, 0), first, second, before, last, (below, 0)]
    return pl.pallas_call(
        functools.partial(edge_kernel, with_wide),
        grid=(columns // LANES,),
        in_specs=[rows_spec(1, cols, at) for _, at in picks] + [pl.BlockSpec((rows, cols, 1), lambda j: (0, 0, 0))],
        out_specs=[rows_spec(out.shape[0], cols) for out in outs],
        out_shape=outs,
        cost_estimate=pl.CostEstimate(flops=16 * above.size, bytes_accessed=36 * above.size, transcendentals=0),
        name="stencil_edge",
    )(*[array for array, _ in picks], kappa)


def halo(first, last):
    count = lax.axis_size("space")
    forward = [(i, i + 1) for i in range(count - 1)]
    backward = [(target, source) for source, target in forward]
    above = lax.ppermute(last, "space", forward)
    below = lax.ppermute(first, "space", backward)
    return above, below


def gather_pieces(own):
    count = lax.axis_size("species")
    pieces = {0: own}
    for d in range(2, count, 2):
        pieces[d] = xor_swap(own, "species", d)
    for d in range(0, count, 2):
        pieces[d + 1] = xor_swap(pieces[d], "species", 1)
    return [pieces[d] for d in range(count)]


def prior_kernel(pieces, *refs):
    tree_ref, out_ref = refs[2 * pieces], refs[2 * pieces + 1]
    total = None
    for at in range(pieces):
        part = jnp.dot(refs[at][...], refs[pieces + at][...], preferred_element_type=jnp.float32)
        total = part if total is None else total + part
    out_ref[...] = tree_ref[...] - total


def minus_prior(tree, pieces, weights, row_of, block):
    plots, columns = pieces[0].shape
    count = len(pieces)
    held = pl.BlockSpec((block, columns), lambda i: (row_of(i), 0))
    return pl.pallas_call(
        functools.partial(prior_kernel, count),
        grid=(plots // block,),
        in_specs=[pl.BlockSpec((block, columns), lambda i: (i, 0))] * count
        + [pl.BlockSpec((columns, columns), lambda i: (0, 0))] * count
        + [held],
        out_specs=held,
        out_shape=jax.ShapeDtypeStruct(tree.shape, tree.dtype),
        input_output_aliases={2 * count: 0},
        cost_estimate=pl.CostEstimate(
            flops=2 * count * plots * columns * columns, bytes_accessed=16 * plots * columns, transcendentals=0
        ),
        name="prior",
    )(*pieces, *weights, tree)


def sum_over_space(blocks, scale):
    _, block_rows, columns = blocks.shape
    count = lax.axis_size("space")
    outer = count // 2
    per_piece = count // lax.axis_size("species")
    me, mine = lax.axis_index("space"), lax.axis_index("species")
    split = max(16, block_rows * 11 // 16 // 16 * 16)

    def block(target, low, high):
        slot = ((target // per_piece) ^ mine) * per_piece + target % per_piece
        return lax.dynamic_slice(blocks, (slot, low, 0), (1, high - low, columns))

    def pair(low, high, a, b):
        return block(me ^ (2 * a + b), low, high)

    wide = lambda value: value.astype(jnp.float32)
    near_send = jnp.concatenate([pair(0, split, a, 1) for a in range(outer)], axis=0)
    near = xor_swap(near_send, "space", 1)
    far_send = [
        jnp.concatenate([pair(split, block_rows, a, b) for b in range(2)], axis=0) for a in range(1, outer)
    ]
    far = [xor_swap(far_send[a - 1], "space", 2 * a) for a in range(1, outer)]
    near_sum = [wide(pair(0, split, a, 0)[0]) + wide(near[a]) for a in range(outer)]
    near_low = [value.astype(jnp.bfloat16) for value in near_sum]
    near_far = [xor_swap(near_low[a], "space", 2 * a) for a in range(1, outer)]
    far_sum = [wide(pair(split, block_rows, 0, b)[0]) for b in range(2)]
    for part in far:
        far_sum = [far_sum[b] + wide(part[b]) for b in range(2)]
    far_near = xor_swap(far_sum[1].astype(jnp.bfloat16), "space", 1)
    first = near_sum[0]
    for part in near_far:
        first = first + wide(part)
    second = far_sum[0] + wide(far_near)
    return jnp.concatenate([first, second], axis=0) * scale


def shards(effects, kappa_sq, growth, tree_species, tree_counts, noise_precision, species_precision):
    rows, cols, columns = effects.shape
    plots = rows * cols
    slots = growth.shape[2]
    space_count = lax.axis_size("space")
    species_count = lax.axis_size("species")
    mine = lax.axis_index("species")
    kappa = kappa_sq.reshape(rows, cols, 1)
    flat = lambda value: value.reshape(-1, columns)
    above, below = halo(effects[:1], effects[rows - 1 :])
    mid_low, mid_wide = stencil_mid(effects, [], kappa, True)
    mid_pieces = gather_pieces(flat(mid_low))

    tree, tree_parts = None, next(n for n in (3, 2, 1) if rows % n == 0)

    def tree_part(at, before):
        length = plots // tree_parts
        return tree_term(
            effects.reshape(plots, columns),
            growth.reshape(plots, slots),
            tree_species.reshape(plots, slots),
            tree_counts.reshape(plots),
            noise_precision,
            mine * columns,
            at * length,
            length,
            before,
        )

    for at in range(tree_parts):
        tree = tree_part(at, tree)

    edge_low, top_wide, bottom_wide = stencil_edge(
        above, (effects, 0), (effects, 1), (effects, rows - 2), (effects, rows - 1), below, kappa, True
    )
    edge_pieces = gather_pieces(flat(edge_low))
    above_k, below_k = halo(top_wide, bottom_wide)

    (spatial_mid,) = stencil_mid(mid_wide, [top_wide, bottom_wide], kappa, False)
    spatial_mid_pieces = gather_pieces(flat(spatial_mid))

    def product(left, right):
        return lax.dot_general(left, right, (((0,), (0,)), ((), ())), preferred_element_type=jnp.float32)

    grams = []
    for d in range(species_count):
        part = product(mid_pieces[d], mid_pieces[0]) + product(edge_pieces[d], edge_pieces[0])
        grams.append(part.astype(jnp.bfloat16))
    blocks = jnp.stack(grams).reshape(space_count, -1, columns)
    gram = sum_over_space(blocks, -0.5 / (plots * space_count))

    (spatial_edge,) = stencil_edge(
        above_k, (top_wide, 0), (mid_wide, 0), (mid_wide, rows - 3), (bottom_wide, 0), below_k, kappa, False
    )
    spatial_edge_pieces = gather_pieces(flat(spatial_edge))
    weights = [
        lax.dynamic_slice(species_precision, ((mine ^ d) * columns, 0), (columns, columns))
        for d in range(species_count)
    ]
    grad = minus_prior(tree, spatial_mid_pieces, weights, lambda i: i + 1, cols)
    grad = minus_prior(grad, spatial_edge_pieces, weights, lambda i: i * (rows - 1), cols)
    return (grad.reshape(rows, cols, columns), gram)


def solution(mesh):
    return jax.shard_map(
        shards,
        mesh=mesh,
        in_specs=(
            P("space", None, "species"),
            P("space", None),
            P("space", None, None),
            P("space", None, None),
            P("space", None),
            P("species"),
            P(None, "species"),
        ),
        out_specs=(P("space", None, "species"), P("space", "species")),
        check_vma=False,
    )
```

```python
import functools

import jax
import jax.numpy as jnp
from jax import lax
from jax.experimental import pallas as pl
from jax.experimental.pallas import tpu as pltpu
from jax.sharding import PartitionSpec as P


LANES = 128


def xor_swap(value, axis, mask):
    count = lax.axis_size(axis)
    return lax.ppermute(value, axis, [(i, i ^ mask) for i in range(count)])


def tree_kernel(groups, first_block, first_ref, effects_ref, growth_ref, species_ref, counts_ref, noise_ref, *rest):
    out_ref = rest[-1]
    rows, slots = growth_ref.shape
    bits = LANES.bit_length() - 1
    codes = groups * 8
    low_iota = lax.broadcasted_iota(jnp.int32, (LANES, slots), 0).astype(jnp.bfloat16)
    code_iota = lax.broadcasted_iota(jnp.int32, (codes, slots), 0).astype(jnp.bfloat16)
    slot_iota = lax.broadcasted_iota(jnp.int32, (8, slots), 1)
    row_iota = lax.broadcasted_iota(jnp.int32, (8, slots), 0)
    one, zero = jnp.bfloat16(1.0), jnp.bfloat16(0.0)
    first_column = first_ref[3]
    base, per_row = (first_block + pl.program_id(0)) * rows, counts_ref.shape[1]

    def step(index, carry):
        at = pl.ds(pl.multiple_of(index * 8, 8), 8)
        local = species_ref[at, :] - first_column
        group = local >> bits
        grid_row, grid_col = (base + index * 8) // per_row, (base + index * 8) % per_row
        counts = jnp.full((8, slots), counts_ref[grid_row, grid_col])
        for plot in range(1, 8):
            counts = jnp.where(row_iota == plot, counts_ref[grid_row, grid_col + plot], counts)
        valid = (slot_iota < counts) & (group >= 0) & (group < groups)
        code = jnp.where(valid, group * 8 + row_iota, -1).astype(jnp.float32)
        low = (local & (LANES - 1)).astype(jnp.float32)
        value = growth_ref[at, :].astype(jnp.bfloat16).astype(jnp.float32)
        lefts, rights = [], []
        for plot in range(8):
            low_row = jnp.broadcast_to(low[plot : plot + 1], (LANES, slots)).astype(jnp.bfloat16)
            code_row = jnp.broadcast_to(code[plot : plot + 1], (codes, slots)).astype(jnp.bfloat16)
            value_row = jnp.broadcast_to(value[plot : plot + 1], (codes, slots)).astype(jnp.bfloat16)
            match = code_row == code_iota
            rights.append(jnp.where(low_row == low_iota, one, zero))
            lefts.append(
                jnp.concatenate([jnp.where(match, value_row, zero), jnp.where(match, one, zero)], axis=0)
            )
        sums = lax.dot_general(
            jnp.concatenate(rights, axis=1),
            jnp.concatenate(lefts, axis=1),
            (((1,), (1,)), ((), ())),
            preferred_element_type=jnp.float32,
        ).T
        for group_at in range(groups):
            cols = pl.ds(group_at * LANES, LANES)
            growth_sum = sums[group_at * 8 : group_at * 8 + 8]
            tally = sums[codes + group_at * 8 : codes + group_at * 8 + 8]
            out_ref[at, cols] = noise_ref[:, cols] * (growth_sum - tally * effects_ref[at, cols])
        return carry

    lax.fori_loop(0, rows // 8, step, 0, unroll=16)


def tree_term(effects, growth, species, counts, noise, ids, start, length, before):
    plots, columns = effects.shape
    slots = growth.shape[1]
    block = 128
    first = start // block
    row = lambda width: pl.BlockSpec((block, width), lambda i: (first + i, 0))
    held = [] if before is None else [before]
    return pl.pallas_call(
        functools.partial(tree_kernel, columns // LANES, first),
        grid=(length // block,),
        in_specs=[
            pl.BlockSpec(memory_space=pltpu.SMEM),
            row(columns),
            row(slots),
            row(slots),
            pl.BlockSpec(memory_space=pltpu.SMEM),
            pl.BlockSpec((1, columns), lambda i: (0, 0)),
        ]
        + [pl.BlockSpec(memory_space=pl.ANY)] * len(held),
        out_specs=row(columns),
        out_shape=jax.ShapeDtypeStruct((plots, columns), jnp.float32),
        input_output_aliases={6: 0} if held else {},
        cost_estimate=pl.CostEstimate(
            flops=2 * length * slots * 64 * 128, bytes_accessed=8 * length * (slots + columns), transcendentals=0
        ),
        compiler_params=pltpu.CompilerParams(vmem_limit_bytes=8 << 20),
        name="tree_term",
    )(ids, effects, growth, species, counts, noise.reshape(1, columns), *held)


def k_row(above, centre, below, kappa):
    at = lax.broadcasted_iota(jnp.int32, centre.shape, 0)
    last = centre.shape[0] - 1
    left = jnp.where(at == 0, 0.0, pltpu.roll(centre, 1, axis=0))
    right = jnp.where(at == last, 0.0, pltpu.roll(centre, last, axis=0))
    return (kappa + 4.0) * centre - (below + above + right + left)


def mid_kernel(rows, with_wide, *refs):
    if with_wide:
        x_ref, kappa_ref, low_ref, wide_ref = refs
        get = lambda r: x_ref[r]
    else:
        x_ref, top_ref, bottom_ref, kappa_ref, low_ref = refs
        get = lambda r: top_ref[0] if r == 0 else bottom_ref[0] if r == rows - 1 else x_ref[r - 1]
    kappa = kappa_ref[...].T
    for r in range(1, rows - 1):
        value = k_row(get(r - 1), get(r), get(r + 1), kappa[:, r : r + 1])
        low_ref[r - 1] = value.astype(low_ref.dtype)
        if with_wide:
            wide_ref[r - 1] = value


def edge_kernel(with_wide, above_ref, first_ref, second_ref, before_ref, last_ref, below_ref, kappa_ref, *outs):
    rows = kappa_ref.shape[0]
    kappa = kappa_ref[...].T
    top = k_row(above_ref[0], first_ref[0], second_ref[0], kappa[:, :1])
    bottom = k_row(before_ref[0], last_ref[0], below_ref[0], kappa[:, rows - 1 :])
    for at, value in enumerate((top, bottom)):
        outs[0][at] = value.astype(outs[0].dtype)
        if with_wide:
            outs[1 + at][0] = value


def rows_spec(count, cols, first=0):
    return pl.BlockSpec((count, cols, LANES), lambda j: (first // count, 0, j))


def stencil_mid(x, edges, kappa, with_wide):
    rows, cols = kappa.shape
    columns = x.shape[2]
    shape = (rows - 2, cols, columns)
    outs = [jax.ShapeDtypeStruct(shape, jnp.bfloat16)]
    if with_wide:
        outs.append(jax.ShapeDtypeStruct(shape, jnp.float32))
    arrays = [x, *edges]
    return pl.pallas_call(
        functools.partial(mid_kernel, rows, with_wide),
        grid=(columns // LANES,),
        in_specs=[rows_spec(a.shape[0], cols) for a in arrays] + [pl.BlockSpec((rows, cols), lambda j: (0, 0))],
        out_specs=[rows_spec(rows - 2, cols) for _ in outs],
        out_shape=outs,
        cost_estimate=pl.CostEstimate(flops=8 * x.size, bytes_accessed=10 * x.size, transcendentals=0),
        compiler_params=pltpu.CompilerParams(vmem_limit_bytes=10 << 20),
        name="stencil_mid",
    )(*arrays, kappa)


def stencil_edge(above, first, second, before, last, below, kappa, with_wide):
    rows, cols = kappa.shape
    columns = above.shape[2]
    outs = [jax.ShapeDtypeStruct((2, cols, columns), jnp.bfloat16)]
    if with_wide:
        outs += [jax.ShapeDtypeStruct((1, cols, columns), jnp.float32)] * 2
    picks = [(above, 0), first, second, before, last, (below, 0)]
    return pl.pallas_call(
        functools.partial(edge_kernel, with_wide),
        grid=(columns // LANES,),
        in_specs=[rows_spec(1, cols, at) for _, at in picks] + [pl.BlockSpec((rows, cols), lambda j: (0, 0))],
        out_specs=[rows_spec(out.shape[0], cols) for out in outs],
        out_shape=outs,
        cost_estimate=pl.CostEstimate(flops=16 * above.size, bytes_accessed=36 * above.size, transcendentals=0),
        compiler_params=pltpu.CompilerParams(vmem_limit_bytes=10 << 20),
        name="stencil_edge",
    )(*[array for array, _ in picks], kappa)


def halo(first, last):
    count = lax.axis_size("space")
    forward = [(i, i + 1) for i in range(count - 1)]
    backward = [(target, source) for source, target in forward]
    above = lax.ppermute(last, "space", forward)
    below = lax.ppermute(first, "space", backward)
    return above, below


def gather_pieces(own):
    count = lax.axis_size("species")
    pieces = {0: own}
    for d in range(2, count, 2):
        pieces[d] = xor_swap(own, "species", d)
    for d in range(0, count, 2):
        pieces[d + 1] = xor_swap(pieces[d], "species", 1)
    return [pieces[d] for d in range(count)]


def prior_kernel(pieces, ids_ref, *refs):
    tree_ref, out_ref = refs[2 * pieces], refs[2 * pieces + 1]
    total = None
    for at in range(pieces):
        part = jnp.dot(refs[at][...], refs[pieces + at][...], preferred_element_type=jnp.float32)
        total = part if total is None else total + part
    out_ref[...] = tree_ref[...] - total


def minus_prior(tree, pieces, precision, ids, row_of, block):
    plots, columns = pieces[0].shape
    count = len(pieces)
    held = pl.BlockSpec((block, columns), lambda i, ids: (row_of(i), 0))
    weight = lambda d: pl.BlockSpec((columns, columns), lambda i, ids: (ids[0] ^ d, 0))
    return pl.pallas_call(
        functools.partial(prior_kernel, count),
        grid_spec=pltpu.PrefetchScalarGridSpec(
            num_scalar_prefetch=1,
            grid=(plots // block,),
            in_specs=[pl.BlockSpec((block, columns), lambda i, ids: (i, 0))] * count
            + [weight(d) for d in range(count)]
            + [held],
            out_specs=held,
        ),
        out_shape=jax.ShapeDtypeStruct(tree.shape, tree.dtype),
        input_output_aliases={2 * count + 1: 0},
        cost_estimate=pl.CostEstimate(
            flops=2 * count * plots * columns * columns, bytes_accessed=16 * plots * columns, transcendentals=0
        ),
        compiler_params=pltpu.CompilerParams(vmem_limit_bytes=16 << 20),
        name="prior",
    )(ids, *pieces, *([precision] * count), tree)


def pick_kernel(split, ids_ref, blocks_ref, *outs):
    slots = blocks_ref.shape[0]
    outer = slots // 2
    mine, me, per_piece = ids_ref[0], ids_ref[1], ids_ref[2]
    near_send, near_own, far_own, far_sends = outs[0], outs[1], outs[2], outs[3:]
    for a in range(outer):
        for b in range(2):
            target = me ^ (2 * a + b)
            slot = ((target // per_piece) ^ mine) * per_piece + target % per_piece
            (near_send if b else near_own)[a] = blocks_ref[slot, :split]
            (far_sends[a - 1] if a else far_own)[b] = blocks_ref[slot, split:]


def sum_over_space(blocks, scale, ids):
    slots, block_rows, columns = blocks.shape
    outer = slots // 2
    split = max(16, block_rows * 11 // 16 // 16 * 16)
    shape = lambda count, rows: jax.ShapeDtypeStruct((count, rows, columns), blocks.dtype)
    near_send, near_own, far_own, *far_send = pl.pallas_call(
        functools.partial(pick_kernel, split),
        in_specs=[pl.BlockSpec(memory_space=pltpu.SMEM), pl.BlockSpec(memory_space=pltpu.VMEM)],
        out_shape=[shape(outer, split)] * 2 + [shape(2, block_rows - split)] * outer,
        cost_estimate=pl.CostEstimate(flops=0, bytes_accessed=4 * blocks.size, transcendentals=0),
        compiler_params=pltpu.CompilerParams(vmem_limit_bytes=10 << 20),
        name="pick",
    )(ids, blocks)
    wide = lambda value: value.astype(jnp.float32)
    near = xor_swap(near_send, "space", 1)
    far = [xor_swap(far_send[a - 1], "space", 2 * a) for a in range(1, outer)]
    near_sum = [wide(near_own[a]) + wide(near[a]) for a in range(outer)]
    near_low = [value.astype(jnp.bfloat16) for value in near_sum]
    near_far = [xor_swap(near_low[a], "space", 2 * a) for a in range(1, outer)]
    far_sum = [wide(far_own[b]) for b in range(2)]
    for part in far:
        far_sum = [far_sum[b] + wide(part[b]) for b in range(2)]
    far_near = xor_swap(far_sum[1].astype(jnp.bfloat16), "space", 1)
    first = near_sum[0]
    for part in near_far:
        first = first + wide(part)
    second = far_sum[0] + wide(far_near)
    return jnp.concatenate([first, second], axis=0) * scale


def shards(effects, kappa_sq, growth, tree_species, tree_counts, noise_precision, species_precision):
    rows, cols, columns = effects.shape
    plots = rows * cols
    slots = growth.shape[2]
    space_count = lax.axis_size("space")
    species_count = lax.axis_size("species")
    mine = lax.axis_index("species")
    kappa = kappa_sq
    ids = jnp.stack([mine, lax.axis_index("space"), jnp.int32(space_count // species_count), mine * columns])
    effects, ids = lax.optimization_barrier((effects, ids))
    flat = lambda value: value.reshape(-1, columns)
    above, below = halo(effects[:1], effects[rows - 1 :])
    mid_low, mid_wide = stencil_mid(effects, [], kappa, True)
    mid_pieces = gather_pieces(flat(mid_low))

    tree, tree_parts = None, next(n for n in (3, 2, 1) if rows % n == 0)

    def tree_part(at, before):
        length = plots // tree_parts
        return tree_term(
            effects.reshape(plots, columns),
            growth.reshape(plots, slots),
            tree_species.reshape(plots, slots),
            tree_counts,
            noise_precision,
            ids,
            at * length,
            length,
            before,
        )

    for at in range(tree_parts):
        tree = tree_part(at, tree)

    edge_low, top_wide, bottom_wide = stencil_edge(
        above, (effects, 0), (effects, 1), (effects, rows - 2), (effects, rows - 1), below, kappa, True
    )
    edge_pieces = gather_pieces(flat(edge_low))
    above_k, below_k = halo(top_wide, bottom_wide)

    (spatial_mid,) = stencil_mid(mid_wide, [top_wide, bottom_wide], kappa, False)
    spatial_mid_pieces = gather_pieces(flat(spatial_mid))

    def product(left, right):
        return lax.dot_general(left, right, (((0,), (0,)), ((), ())), preferred_element_type=jnp.float32)

    grams = []
    for d in range(species_count):
        part = product(mid_pieces[d], mid_pieces[0]) + product(edge_pieces[d], edge_pieces[0])
        grams.append(part.astype(jnp.bfloat16))
    blocks = jnp.stack(grams).reshape(space_count, -1, columns)
    gram = sum_over_space(blocks, -0.5 / (plots * space_count), ids)

    (spatial_edge,) = stencil_edge(
        above_k, (top_wide, 0), (mid_wide, 0), (mid_wide, rows - 3), (bottom_wide, 0), below_k, kappa, False
    )
    spatial_edge_pieces = gather_pieces(flat(spatial_edge))
    grad = minus_prior(tree, spatial_mid_pieces, species_precision, ids, lambda i: i + 1, cols)
    grad = minus_prior(grad, spatial_edge_pieces, species_precision, ids, lambda i: i * (rows - 1), cols)
    return (grad.reshape(rows, cols, columns), gram)


def solution(mesh):
    return jax.shard_map(
        shards,
        mesh=mesh,
        in_specs=(
            P("space", None, "species"),
            P("space", None),
            P("space", None, None),
            P("space", None, None),
            P("space", None),
            P("species"),
            P(None, "species"),
        ),
        out_specs=(P("space", None, "species"), P("space", "species")),
        check_vma=False,
    )
```

```python
import functools

import jax
import jax.numpy as jnp
from jax import lax
from jax.experimental import pallas as pl
from jax.experimental.pallas import tpu as pltpu
from jax.sharding import PartitionSpec as P


LANES = 128


def xor_swap(value, axis, mask):
    count = lax.axis_size(axis)
    return lax.ppermute(value, axis, [(i, i ^ mask) for i in range(count)])


def tree_kernel(groups, first_block, first_ref, effects_ref, growth_ref, species_ref, counts_ref, noise_ref, *rest):
    out_ref = rest[-1]
    rows, slots = growth_ref.shape
    bits = LANES.bit_length() - 1
    codes = groups * 8
    low_iota = lax.broadcasted_iota(jnp.int32, (LANES, slots), 0).astype(jnp.bfloat16)
    code_iota = lax.broadcasted_iota(jnp.int32, (codes, slots), 0).astype(jnp.bfloat16)
    slot_iota = lax.broadcasted_iota(jnp.int32, (8, slots), 1)
    row_iota = lax.broadcasted_iota(jnp.int32, (8, slots), 0)
    one, zero = jnp.bfloat16(1.0), jnp.bfloat16(0.0)
    first_column = first_ref[3]
    base, per_row = (first_block + pl.program_id(0)) * rows, counts_ref.shape[1]

    def step(index, carry):
        at = pl.ds(pl.multiple_of(index * 8, 8), 8)
        local = species_ref[at, :] - first_column
        group = local >> bits
        grid_row, grid_col = (base + index * 8) // per_row, (base + index * 8) % per_row
        counts = jnp.full((8, slots), counts_ref[grid_row, grid_col])
        for plot in range(1, 8):
            counts = jnp.where(row_iota == plot, counts_ref[grid_row, grid_col + plot], counts)
        valid = (slot_iota < counts) & (group >= 0) & (group < groups)
        code = jnp.where(valid, group * 8 + row_iota, -1).astype(jnp.float32)
        low = (local & (LANES - 1)).astype(jnp.float32)
        value = growth_ref[at, :].astype(jnp.bfloat16).astype(jnp.float32)
        lefts, rights = [], []
        for plot in range(8):
            low_row = jnp.broadcast_to(low[plot : plot + 1], (LANES, slots)).astype(jnp.bfloat16)
            code_row = jnp.broadcast_to(code[plot : plot + 1], (codes, slots)).astype(jnp.bfloat16)
            value_row = jnp.broadcast_to(value[plot : plot + 1], (codes, slots)).astype(jnp.bfloat16)
            match = code_row == code_iota
            rights.append(jnp.where(low_row == low_iota, one, zero))
            lefts.append(
                jnp.concatenate([jnp.where(match, value_row, zero), jnp.where(match, one, zero)], axis=0)
            )
        sums = lax.dot_general(
            jnp.concatenate(rights, axis=1),
            jnp.concatenate(lefts, axis=1),
            (((1,), (1,)), ((), ())),
            preferred_element_type=jnp.float32,
        ).T
        for group_at in range(groups):
            cols = pl.ds(group_at * LANES, LANES)
            growth_sum = sums[group_at * 8 : group_at * 8 + 8]
            tally = sums[codes + group_at * 8 : codes + group_at * 8 + 8]
            out_ref[at, cols] = noise_ref[:, cols] * (growth_sum - tally * effects_ref[at, cols])
        return carry

    lax.fori_loop(0, rows // 8, step, 0, unroll=16)


def tree_term(effects, growth, species, counts, noise, ids, start, length, before):
    plots, columns = effects.shape
    slots = growth.shape[1]
    block = 128
    first = start // block
    row = lambda width: pl.BlockSpec((block, width), lambda i: (first + i, 0))
    held = [] if before is None else [before]
    return pl.pallas_call(
        functools.partial(tree_kernel, columns // LANES, first),
        grid=(length // block,),
        in_specs=[
            pl.BlockSpec(memory_space=pltpu.SMEM),
            row(columns),
            row(slots),
            row(slots),
            pl.BlockSpec(memory_space=pltpu.SMEM),
            pl.BlockSpec((1, columns), lambda i: (0, 0)),
        ]
        + [pl.BlockSpec(memory_space=pl.ANY)] * len(held),
        out_specs=row(columns),
        out_shape=jax.ShapeDtypeStruct((plots, columns), jnp.float32),
        input_output_aliases={6: 0} if held else {},
        cost_estimate=pl.CostEstimate(
            flops=2 * length * slots * 64 * 128, bytes_accessed=8 * length * (slots + columns), transcendentals=0
        ),
        compiler_params=pltpu.CompilerParams(vmem_limit_bytes=8 << 20),
        name="tree_term",
    )(ids, effects, growth, species, counts, noise.reshape(1, columns), *held)


def k_row(above, centre, below, kappa):
    at = lax.broadcasted_iota(jnp.int32, centre.shape, 0)
    last = centre.shape[0] - 1
    left = jnp.where(at == 0, 0.0, pltpu.roll(centre, 1, axis=0))
    right = jnp.where(at == last, 0.0, pltpu.roll(centre, last, axis=0))
    return (kappa + 4.0) * centre - (below + above + right + left)


def mid_kernel(rows, with_wide, *refs):
    if with_wide:
        x_ref, kappa_ref, low_ref, wide_ref = refs
        get = lambda r: x_ref[r]
    else:
        x_ref, top_ref, bottom_ref, kappa_ref, low_ref = refs
        get = lambda r: top_ref[0] if r == 0 else bottom_ref[0] if r == rows - 1 else x_ref[r - 1]
    kappa = kappa_ref[...].T
    for r in range(1, rows - 1):
        value = k_row(get(r - 1), get(r), get(r + 1), kappa[:, r : r + 1])
        low_ref[r - 1] = value.astype(low_ref.dtype)
        if with_wide:
            wide_ref[r - 1] = value


def edge_kernel(with_wide, above_ref, first_ref, second_ref, before_ref, last_ref, below_ref, kappa_ref, *outs):
    rows = kappa_ref.shape[0]
    kappa = kappa_ref[...].T
    top = k_row(above_ref[0], first_ref[0], second_ref[0], kappa[:, :1])
    bottom = k_row(before_ref[0], last_ref[0], below_ref[0], kappa[:, rows - 1 :])
    for at, value in enumerate((top, bottom)):
        outs[0][at] = value.astype(outs[0].dtype)
        if with_wide:
            outs[1 + at][0] = value


def rows_spec(count, cols, first=0):
    return pl.BlockSpec((count, cols, LANES), lambda j: (first // count, 0, j))


def stencil_mid(x, edges, kappa, with_wide):
    rows, cols = kappa.shape
    columns = x.shape[2]
    shape = (rows - 2, cols, columns)
    outs = [jax.ShapeDtypeStruct(shape, jnp.bfloat16)]
    if with_wide:
        outs.append(jax.ShapeDtypeStruct(shape, jnp.float32))
    arrays = [x, *edges]
    return pl.pallas_call(
        functools.partial(mid_kernel, rows, with_wide),
        grid=(columns // LANES,),
        in_specs=[rows_spec(a.shape[0], cols) for a in arrays] + [pl.BlockSpec((rows, cols), lambda j: (0, 0))],
        out_specs=[rows_spec(rows - 2, cols) for _ in outs],
        out_shape=outs,
        cost_estimate=pl.CostEstimate(flops=8 * x.size, bytes_accessed=10 * x.size, transcendentals=0),
        compiler_params=pltpu.CompilerParams(vmem_limit_bytes=10 << 20),
        name="stencil_mid",
    )(*arrays, kappa)


def stencil_edge(above, first, second, before, last, below, kappa, with_wide):
    rows, cols = kappa.shape
    columns = above.shape[2]
    outs = [jax.ShapeDtypeStruct((2, cols, columns), jnp.bfloat16)]
    if with_wide:
        outs += [jax.ShapeDtypeStruct((1, cols, columns), jnp.float32)] * 2
    picks = [(above, 0), first, second, before, last, (below, 0)]
    return pl.pallas_call(
        functools.partial(edge_kernel, with_wide),
        grid=(columns // LANES,),
        in_specs=[rows_spec(1, cols, at) for _, at in picks] + [pl.BlockSpec((rows, cols), lambda j: (0, 0))],
        out_specs=[rows_spec(out.shape[0], cols) for out in outs],
        out_shape=outs,
        cost_estimate=pl.CostEstimate(flops=16 * above.size, bytes_accessed=36 * above.size, transcendentals=0),
        compiler_params=pltpu.CompilerParams(vmem_limit_bytes=10 << 20),
        name="stencil_edge",
    )(*[array for array, _ in picks], kappa)


def halo(first, last):
    count = lax.axis_size("space")
    forward = [(i, i + 1) for i in range(count - 1)]
    backward = [(target, source) for source, target in forward]
    above = lax.ppermute(last, "space", forward)
    below = lax.ppermute(first, "space", backward)
    return above, below


def gather_pieces(own):
    count = lax.axis_size("species")
    pieces = {0: own}
    for d in range(2, count, 2):
        pieces[d] = xor_swap(own, "species", d)
    for d in range(0, count, 2):
        pieces[d + 1] = xor_swap(pieces[d], "species", 1)
    return [pieces[d] for d in range(count)]


def prior_kernel(count, chunks, ids_ref, *refs):
    pieces, precision_ref, tree_ref = refs[:count], refs[count], refs[count + 1]
    out_ref, held, in_sem, out_sem = refs[count + 2 :]
    columns = precision_ref.shape[1]
    width = columns // 2
    depth = pieces[0].shape[1]

    def copies(at, outward):
        made, row = [], 0
        for part, (first, length) in enumerate(chunks[at]):
            here = held.at[at, pl.ds(row, length)]
            there = pl.ds(first, length)
            if outward:
                made.append(pltpu.make_async_copy(here, out_ref.at[there], out_sem.at[at, part]))
            else:
                made.append(pltpu.make_async_copy(tree_ref.at[there], here, in_sem.at[at, part]))
            row += length
        return made

    for at in range(len(chunks)):
        for copy in copies(at, False):
            copy.start()
    rows = held.shape[1]
    for at in range(len(chunks)):
        left = jnp.concatenate([piece[at * rows : (at + 1) * rows, :] for piece in pieces], axis=1)
        for half in range(2):
            cols = slice(half * width, (half + 1) * width)
            firsts = [pl.multiple_of((ids_ref[0] ^ d) * depth, depth) for d in range(count)]
            weight = jnp.concatenate([precision_ref[pl.ds(first, depth), cols] for first in firsts], axis=0)
            total = jnp.dot(left, weight, preferred_element_type=jnp.float32)
            if half == 0:
                for copy in copies(at, False):
                    copy.wait()
            held[at, :, cols] -= total
        for copy in copies(at, True):
            copy.start()
    for at in range(len(chunks)):
        for copy in copies(at, True):
            copy.wait()


def minus_prior(tree, pieces, precision, ids, chunks):
    plots, columns = pieces[0].shape
    count = len(pieces)
    rows = plots // len(chunks)
    parts = len(chunks[0])
    vmem = pl.BlockSpec(memory_space=pltpu.VMEM)
    hbm = pl.BlockSpec(memory_space=pltpu.HBM)
    return pl.pallas_call(
        functools.partial(prior_kernel, count, chunks),
        in_specs=[pl.BlockSpec(memory_space=pltpu.SMEM)] + [vmem] * (count + 1) + [hbm],
        out_specs=hbm,
        out_shape=jax.ShapeDtypeStruct(tree.shape, tree.dtype),
        input_output_aliases={count + 2: 0},
        scratch_shapes=[
            pltpu.VMEM((len(chunks), rows, columns), jnp.float32),
            pltpu.SemaphoreType.DMA((len(chunks), parts)),
            pltpu.SemaphoreType.DMA((len(chunks), parts)),
        ],
        cost_estimate=pl.CostEstimate(
            flops=2 * count * plots * columns * columns, bytes_accessed=16 * plots * columns, transcendentals=0
        ),
        compiler_params=pltpu.CompilerParams(vmem_limit_bytes=16 << 20),
        name="prior",
    )(ids, *pieces, precision, tree)


def pick_kernel(split, ids_ref, blocks_ref, *outs):
    slots = blocks_ref.shape[0]
    outer = slots // 2
    mine, me, per_piece = ids_ref[0], ids_ref[1], ids_ref[2]
    near_send, near_own, far_own, far_sends = outs[0], outs[1], outs[2], outs[3:]
    for a in range(outer):
        for b in range(2):
            target = me ^ (2 * a + b)
            slot = ((target // per_piece) ^ mine) * per_piece + target % per_piece
            (near_send if b else near_own)[a] = blocks_ref[slot, :split]
            (far_sends[a - 1] if a else far_own)[b] = blocks_ref[slot, split:]


def sum_over_space(blocks, scale, ids):
    slots, block_rows, columns = blocks.shape
    outer = slots // 2
    split = max(16, block_rows * 11 // 16 // 16 * 16)
    shape = lambda count, rows: jax.ShapeDtypeStruct((count, rows, columns), blocks.dtype)
    near_send, near_own, far_own, *far_send = pl.pallas_call(
        functools.partial(pick_kernel, split),
        in_specs=[pl.BlockSpec(memory_space=pltpu.SMEM), pl.BlockSpec(memory_space=pltpu.VMEM)],
        out_shape=[shape(outer, split)] * 2 + [shape(2, block_rows - split)] * outer,
        cost_estimate=pl.CostEstimate(flops=0, bytes_accessed=4 * blocks.size, transcendentals=0),
        compiler_params=pltpu.CompilerParams(vmem_limit_bytes=10 << 20),
        name="pick",
    )(ids, blocks)
    wide = lambda value: value.astype(jnp.float32)
    near = xor_swap(near_send, "space", 1)
    far = [xor_swap(far_send[a - 1], "space", 2 * a) for a in range(1, outer)]
    near_sum = [wide(near_own[a]) + wide(near[a]) for a in range(outer)]
    near_low = [value.astype(jnp.bfloat16) for value in near_sum]
    near_far = [xor_swap(near_low[a], "space", 2 * a) for a in range(1, outer)]
    far_sum = [wide(far_own[b]) for b in range(2)]
    for part in far:
        far_sum = [far_sum[b] + wide(part[b]) for b in range(2)]
    far_near = xor_swap(far_sum[1].astype(jnp.bfloat16), "space", 1)
    first = near_sum[0]
    for part in near_far:
        first = first + wide(part)
    second = far_sum[0] + wide(far_near)
    return jnp.concatenate([first, second], axis=0) * scale


def shards(effects, kappa_sq, growth, tree_species, tree_counts, noise_precision, species_precision):
    rows, cols, columns = effects.shape
    plots = rows * cols
    slots = growth.shape[2]
    space_count = lax.axis_size("space")
    species_count = lax.axis_size("species")
    mine = lax.axis_index("species")
    kappa = kappa_sq
    ids = jnp.stack([mine, lax.axis_index("space"), jnp.int32(space_count // species_count), mine * columns])
    effects, ids = lax.optimization_barrier((effects, ids))
    flat = lambda value: value.reshape(-1, columns)
    above, below = halo(effects[:1], effects[rows - 1 :])
    mid_low, mid_wide = stencil_mid(effects, [], kappa, True)
    mid_pieces = gather_pieces(flat(mid_low))

    tree, tree_parts = None, next(n for n in (3, 2, 1) if rows % n == 0)

    def tree_part(at, before):
        length = plots // tree_parts
        return tree_term(
            effects.reshape(plots, columns),
            growth.reshape(plots, slots),
            tree_species.reshape(plots, slots),
            tree_counts,
            noise_precision,
            ids,
            at * length,
            length,
            before,
        )

    for at in range(tree_parts):
        tree = tree_part(at, tree)

    edge_low, top_wide, bottom_wide = stencil_edge(
        above, (effects, 0), (effects, 1), (effects, rows - 2), (effects, rows - 1), below, kappa, True
    )
    edge_pieces = gather_pieces(flat(edge_low))
    above_k, below_k = halo(top_wide, bottom_wide)

    (spatial_mid,) = stencil_mid(mid_wide, [top_wide, bottom_wide], kappa, False)
    spatial_mid_pieces = gather_pieces(flat(spatial_mid))

    def product(left, right):
        return lax.dot_general(left, right, (((0,), (0,)), ((), ())), preferred_element_type=jnp.float32)

    grams = []
    for d in range(species_count):
        part = product(mid_pieces[d], mid_pieces[0]) + product(edge_pieces[d], edge_pieces[0])
        grams.append(part.astype(jnp.bfloat16))
    blocks = jnp.stack(grams).reshape(space_count, -1, columns)
    gram = sum_over_space(blocks, -0.5 / (plots * space_count), ids)

    (spatial_edge,) = stencil_edge(
        above_k, (top_wide, 0), (mid_wide, 0), (mid_wide, rows - 3), (bottom_wide, 0), below_k, kappa, False
    )
    spatial_edge_pieces = gather_pieces(flat(spatial_edge))
    middle = (rows - 2) * cols
    half = middle // 2
    chunks = (((cols, half),), ((cols + half, half),))
    grad = minus_prior(tree, spatial_mid_pieces, species_precision, ids, chunks)
    chunks = (((0, cols), (plots - cols, cols)),)
    grad = minus_prior(grad, spatial_edge_pieces, species_precision, ids, chunks)
    return (grad.reshape(rows, cols, columns), gram)


def solution(mesh):
    return jax.shard_map(
        shards,
        mesh=mesh,
        in_specs=(
            P("space", None, "species"),
            P("space", None),
            P("space", None, None),
            P("space", None, None),
            P("space", None),
            P("species"),
            P(None, "species"),
        ),
        out_specs=(P("space", None, "species"), P("space", "species")),
        check_vma=False,
    )
```
